128 devices in a mesh: leaf: 8 (over y_lo, z), front: 16 (over x, y_hi, core).
Axes of the slice: x: 4, y: 4 (y_hi: 2, y_lo: 2; y = y_hi * 2 + y_lo), z: 4, core: 2. Of those that a mesh axis runs over, the one named last changes fastest.
Arguments:
- leaf_fronts: float32 [32768, 4096], P('leaf', 'front'), as said below
- root_front: float32 [4096, 16, 256], P(None, 'front', 'leaf'), as said below
- leaf_order: int32 [8, 16], P('leaf'), may hold values from 0 to 15, each once within a row
- leaf_map: int32 [8, 16], P('leaf'), may hold values from 0 to 15, each once within a row
- root_order: int32 [16], replicated, may hold values from 0 to 15, each once
Outputs:
- leaf_factor: float32 [32768, 4096], P('leaf', 'front')
- root_factor: float32 [4096, 16, 256], P(None, 'front', 'leaf')
The draws below stay inside these ranges and needn't reach their ends.
Inputs may be any that keep to these rules, and one draw needn't show every extreme that they name: `leaf_fronts`: each leaf block of 4096 rows is symmetric and positive definite. `root_front`: symmetric and positive definite. `leaf_order`: each row names every block column once. `leaf_map`: each row names every root block once. `root_order`: names every block column once.
All inputs are finite; a program needn't handle non-finite values.
Results may differ from the reference program's by a relative error of at most 0.00018.
Values sent between devices are 32-bit elements; how exact they have to be, the bound alone decides.
A program may use at most 128 MiB of HBM per device.

```python
import math
import jax
import jax.numpy as jnp
from jax import lax

B = 256
NPIV = 2
RPIV = 1
NBLK = 16
FROWS = 4096
LEAVES = 8


def kernel_front(key, size_order, amplitude):
    key_place, key_nugget = jax.random.split(key, 2)
    places = jax.random.uniform(key_place, (3, size_order), jnp.float32, 0.0, 1.0)
    reach = 4.0 * (12.0 / (8.0 * math.pi * size_order)) ** (1.0 / 3.0)
    squared = jnp.zeros((size_order, size_order), jnp.float32)
    for coord in range(3):
        spacing = places[coord][:, None] - places[coord][None, :]
        squared = squared + spacing * spacing
    kernel = jnp.exp(-jnp.sqrt(squared) / reach)
    nugget = jnp.exp(jax.random.uniform(key_nugget, (size_order,), jnp.float32, math.log(0.2), math.log(0.8)))
    indices = jnp.arange(size_order)
    on_diagonal = indices[:, None] == indices[None, :]
    matrix = kernel + jnp.where(on_diagonal, nugget[:, None], 0.0)
    return amplitude * matrix


def draw_leaf_fronts(key, part):
    split_keys = jax.random.split(key, LEAVES)
    stacked = lax.map(lambda single: kernel_front(single, FROWS, 1.0), split_keys)
    return stacked.reshape(LEAVES * FROWS, FROWS)


def draw_root_front(key, part):
    return kernel_front(jax.random.fold_in(key, 7), FROWS, 0.5 * LEAVES).reshape(FROWS, NBLK, B)


def setup_inputs(seed: int = 0) -> dict:
    keys = jax.random.split(jax.random.key(seed), 6)
    return {
        "leaf_fronts": draw_leaf_fronts(jax.random.fold_in(keys[5], 71), 0),
        "root_front": draw_root_front(jax.random.fold_in(keys[5], 71), 0),
        "leaf_order": jax.vmap(lambda own: jax.random.permutation(own, NBLK))(jax.random.split(keys[2], LEAVES)).reshape((LEAVES, NBLK)).astype(jnp.int32),
        "leaf_map": jax.vmap(lambda own: jax.random.permutation(own, NBLK))(jax.random.split(keys[3], LEAVES)).reshape((LEAVES, NBLK)).astype(jnp.int32),
        "root_order": jax.random.permutation(keys[4], NBLK).astype(jnp.int32),
    }


def invert(permutation):
    block_ids = jnp.arange(permutation.shape[0], dtype=jnp.int32)
    hits = permutation[None, :] == block_ids[:, None]
    return jnp.sum(jnp.where(hits, block_ids[None, :], 0), axis=1).astype(jnp.int32)

def make_panel(raw_column, pivot_block, alive_set, block_size):
    block_count = raw_column.shape[0] // block_size
    tile_stack = raw_column.reshape(block_count, block_size, block_size)
    diag_block = lax.dynamic_index_in_dim(tile_stack, pivot_block, 0, keepdims=False)
    lower_factor = jnp.linalg.cholesky(diag_block)
    solved = lax.linalg.triangular_solve(lower_factor, raw_column, left_side=False, lower=True, transpose_a=True)
    keep_rows = alive_set & (jnp.arange(block_count, dtype=jnp.int32) != pivot_block)
    solved = jnp.where(jnp.repeat(keep_rows, block_size)[:, None], solved, 0.0)
    tile_stack = solved.reshape(block_count, block_size, block_size)
    tile_stack = lax.dynamic_update_index_in_dim(tile_stack, lower_factor, pivot_block, 0)
    return tile_stack.reshape(block_count * block_size, block_size)

def eliminate(matrix, pivot_block, alive_set, block_size):
    block_count = matrix.shape[0] // block_size
    start_row = (pivot_block * block_size).astype(jnp.int32)
    raw_column = lax.dynamic_slice_in_dim(matrix, start_row, block_size, 1)
    factor_panel = make_panel(raw_column, pivot_block, alive_set, block_size)
    outer_term = jnp.dot(factor_panel, factor_panel.T, precision=lax.Precision.HIGHEST)
    column_alive = jnp.repeat(alive_set, block_size)
    updated = jnp.where(column_alive[None, :], matrix - outer_term, matrix)
    updated = lax.dynamic_update_slice_in_dim(updated, factor_panel, start_row, 1)
    return (updated, alive_set & (jnp.arange(block_count, dtype=jnp.int32) != pivot_block))

def final_mask(matrix, alive_set, block_size):
    row_alive = jnp.repeat(alive_set, block_size)
    return jnp.where(row_alive[None, :] & ~row_alive[:, None], 0.0, matrix)

def reference(leaf_fronts, root_front, leaf_order, leaf_map, root_order):
    assembled = root_front.reshape(FROWS, FROWS)
    factored = []
    for leaf_index in range(LEAVES):
        front_rows = leaf_fronts[leaf_index * FROWS:(leaf_index + 1) * FROWS]
        alive_set = jnp.ones((NBLK,), dtype=jnp.bool_)
        for position in range(NPIV):
            front_rows, alive_set = eliminate(front_rows, leaf_order[leaf_index, position], alive_set, B)
        front_rows = final_mask(front_rows, alive_set, B)
        factored.append(front_rows)
        column_alive = jnp.repeat(alive_set, B)
        schur_part = jnp.where(column_alive[None, :], front_rows, 0.0)
        inverse = invert(leaf_map[leaf_index])
        blocks = schur_part.reshape(NBLK, B, NBLK, B)
        placed = jnp.take(jnp.take(blocks, inverse, axis=0), inverse, axis=2)
        assembled = assembled + placed.reshape(FROWS, FROWS)
    root_alive = jnp.ones((NBLK,), dtype=jnp.bool_)
    for position in range(RPIV):
        assembled, root_alive = eliminate(assembled, root_order[position], root_alive, B)
    assembled = final_mask(assembled, root_alive, B)
    return (jnp.concatenate(factored, axis=0), assembled.reshape(FROWS, NBLK, B))
```

```python
import jax
import jax.numpy as jnp
from jax import lax
from jax.sharding import PartitionSpec as P

HIGH = lax.Precision.HIGH


def invert(permutation):
    block_ids = jnp.arange(permutation.shape[0], dtype=jnp.int32)
    hits = permutation[None, :] == block_ids[:, None]
    return jnp.sum(jnp.where(hits, block_ids[None, :], 0), axis=1)


def make_panel(raw_column, pivot_block, alive_set):
    block_size = raw_column.shape[1]
    block_count = raw_column.shape[0] // block_size
    diag_block = lax.dynamic_slice_in_dim(raw_column, pivot_block * block_size, block_size, 0)
    lower = jnp.linalg.cholesky(diag_block)
    solved = lax.linalg.triangular_solve(
        lower, raw_column, left_side=False, lower=True, transpose_a=True
    )
    block_ids = jnp.arange(block_count, dtype=jnp.int32)
    keep = (alive_set & (block_ids != pivot_block))[:, None, None]
    tiles = solved.reshape(block_count, block_size, block_size)
    on_pivot = (block_ids == pivot_block)[:, None, None]
    tiles = jnp.where(on_pivot, lower[None], jnp.where(keep, tiles, 0.0))
    return tiles.reshape(block_count * block_size, block_size)


def block_row(tiles, pivot_block):
    return lax.dynamic_index_in_dim(tiles, pivot_block, 0, keepdims=False)


def shards(leaf_fronts, root_front, leaf_order, leaf_map, root_order):
    order_rows, block_size = leaf_fronts.shape
    block_count = order_rows // block_size
    my_block = lax.axis_index("front")
    leaf_index = lax.axis_index("leaf")
    slice_width = root_front.shape[2]
    block_ids = jnp.arange(block_count, dtype=jnp.int32)
    own_start = my_block * block_size

    tiles = leaf_fronts.reshape(block_count, block_size, block_size)
    first, second = leaf_order[0, 0], leaf_order[0, 1]
    raw_first = lax.all_gather(block_row(tiles, first).T, "front", axis=0, tiled=True)
    raw_second = lax.all_gather(block_row(tiles, second).T, "front", axis=0, tiled=True)
    everything = jnp.ones((block_count,), dtype=jnp.bool_)
    panel_first = make_panel(raw_first, first, everything)
    alive = block_ids != first
    pivot_rows = lax.dynamic_slice_in_dim(panel_first, second * block_size, block_size, 0)
    raw_second = raw_second - jnp.dot(panel_first, pivot_rows.T, precision=HIGH)
    panel_second = make_panel(raw_second, second, alive)
    alive = alive & (block_ids != second)

    own_first = lax.dynamic_slice_in_dim(panel_first, own_start, block_size, 0)
    own_second = lax.dynamic_slice_in_dim(panel_second, own_start, block_size, 0)
    updated = (
        leaf_fronts
        - jnp.dot(panel_first, own_first.T, precision=HIGH)
        - jnp.dot(panel_second, own_second.T, precision=HIGH)
    )
    updated = updated.reshape(block_count, block_size, block_size)
    updated = jnp.where(alive[:, None, None], updated, 0.0)
    leaf_out = jnp.where(
        my_block == first,
        panel_first,
        jnp.where(my_block == second, panel_second, updated.reshape(order_rows, block_size)),
    )

    mine_alive = alive[my_block]
    inverse = invert(leaf_map[0])
    outgoing = jnp.take(jnp.where(mine_alive, updated, 0.0), inverse, axis=0)
    incoming = lax.all_to_all(outgoing, "front", split_axis=0, concat_axis=0, tiled=True)
    gathered = jnp.swapaxes(jnp.take(incoming, inverse, axis=0), 0, 1)
    gathered = gathered.reshape(block_size, order_rows)
    part = lax.psum_scatter(gathered, "leaf", scatter_dimension=0, tiled=True)
    part = part + root_front[:, 0, :].T

    pivot = root_order[0]
    row = lax.dynamic_slice_in_dim(part, pivot * block_size, block_size, 1)
    raw_root = lax.all_gather(row, ("front", "leaf"), axis=0, tiled=True)
    panel = make_panel(raw_root, pivot, everything)
    own = lax.dynamic_slice_in_dim(panel, own_start + leaf_index * slice_width, slice_width, 0)
    part = part - jnp.dot(own, panel.T, precision=HIGH)
    part = part.reshape(slice_width, block_count, block_size)
    part = jnp.where((block_ids != pivot)[None, :, None], part, 0.0)
    part = part.reshape(slice_width, order_rows)
    own_panel = lax.dynamic_slice_in_dim(panel, leaf_index * slice_width, slice_width, 1)
    root_out = jnp.where(my_block == pivot, own_panel, part.T)
    return (leaf_out, root_out[:, None, :])


def solution(mesh):
    return jax.shard_map(
        shards,
        mesh=mesh,
        in_specs=(
            P("leaf", "front"),
            P(None, "front", "leaf"),
            P("leaf", None),
            P("leaf", None),
            P(),
        ),
        out_specs=(P("leaf", "front"), P(None, "front", "leaf")),
        check_vma=False,
    )
```

```python
import jax
import jax.numpy as jnp
from jax import lax
from jax.experimental import pallas as pl
from jax.experimental.pallas import tpu as pltpu
from jax.sharding import PartitionSpec as P

HIGH = lax.Precision.HIGH
HIGHEST = lax.Precision.HIGHEST
STEP = 32
LANES = 128


def invert(permutation):
    block_ids = jnp.arange(permutation.shape[0], dtype=jnp.int32)
    hits = permutation[None, :] == block_ids[:, None]
    return jnp.sum(jnp.where(hits, block_ids[None, :], 0), axis=1).astype(jnp.int32)


def factor_kernel(diag_ref, upper_ref, inverse_ref, work_ref):
    size = diag_ref.shape[0]
    work_ref[:, :size] = diag_ref[...]
    rows = lax.broadcasted_iota(jnp.int32, (size, size), 0)
    lanes = lax.broadcasted_iota(jnp.int32, (size, size), 1)
    work_ref[:, size:] = jnp.where(rows == lanes, 1.0, 0.0)
    row_ids = lax.broadcasted_iota(jnp.int32, (STEP, LANES), 0)
    lane_ids = lax.broadcasted_iota(jnp.int32, (STEP, LANES), 1)
    for start in range(0, size, STEP):
        base = start // LANES * LANES
        tile = work_ref[start : start + STEP, base : base + LANES]
        unit = jnp.where(row_ids == lane_ids, 1.0, 0.0)
        pivots = jnp.ones((STEP, LANES), jnp.float32)
        for k in range(STEP):
            lane = start - base + k
            column = jnp.broadcast_to(tile[:, lane : lane + 1], (STEP, LANES))
            pivot = jnp.broadcast_to(column[k : k + 1, :], (STEP, LANES))
            pivots = jnp.where(row_ids == k, pivot, pivots)
            if k < STEP - 1:
                scaled = jnp.where(row_ids > k, column / pivot, 0.0)
                tile = tile - scaled * tile[k : k + 1, :]
                unit = unit - scaled * unit[k : k + 1, :]
        small = (unit / jnp.sqrt(pivots))[:, :STEP]
        final = jnp.dot(
            small,
            work_ref[start : start + STEP, :],
            precision=HIGHEST,
            preferred_element_type=jnp.float32,
        )
        upper_ref[start : start + STEP, :] = final[:, :size]
        inverse_ref[start : start + STEP, :] = final[:, size:]
        if start + STEP < size:
            below = start + STEP
            update = lax.dot_general(
                final[:, below // LANES * LANES : size],
                final,
                (((0,), (0,)), ((), ())),
                precision=HIGHEST,
                preferred_element_type=jnp.float32,
            )
            skip = below - below // LANES * LANES
            work_ref[below:, :] = work_ref[below:, :] - update[skip:, :]


def factor(diag_block):
    size = diag_block.shape[0]
    shape = jax.ShapeDtypeStruct((size, size), jnp.float32)
    upper, inverse = pl.pallas_call(
        factor_kernel,
        out_shape=(shape, shape),
        scratch_shapes=[pltpu.VMEM((size, 2 * size), jnp.float32)],
        name="factor",
    )(diag_block)
    ids = jnp.arange(size, dtype=jnp.int32)
    lower = jnp.where(ids[:, None] >= ids[None, :], upper.T, 0.0)
    return lower, jnp.where(ids[:, None] >= ids[None, :], inverse, 0.0)


def make_panel(raw_column, pivot_block, alive_set):
    block_size = raw_column.shape[1]
    block_count = raw_column.shape[0] // block_size
    diag_block = lax.dynamic_slice_in_dim(raw_column, pivot_block * block_size, block_size, 0)
    lower, inverse = factor(diag_block)
    solved = jnp.dot(raw_column, inverse.T, precision=HIGHEST)
    block_ids = jnp.arange(block_count, dtype=jnp.int32)
    keep = (alive_set & (block_ids != pivot_block))[:, None, None]
    tiles = solved.reshape(block_count, block_size, block_size)
    on_pivot = (block_ids == pivot_block)[:, None, None]
    tiles = jnp.where(on_pivot, lower[None], jnp.where(keep, tiles, 0.0))
    return tiles.reshape(block_count * block_size, block_size)


def halves(value):
    top = value.astype(jnp.bfloat16)
    return top, (value - top.astype(jnp.float32)).astype(jnp.bfloat16)


def outer(left, right):
    contract = (((1,), (1,)), ((), ()))
    left_top, left_low = halves(left)
    right_top, right_low = halves(right)
    dot = lambda a, b: lax.dot_general(a, b, contract, preferred_element_type=jnp.float32)
    return dot(left_top, right_top) + (dot(left_top, right_low) + dot(left_low, right_top))


def update_kernel(
    flags, place, front_ref, first_ref, second_ref, own_first_ref, own_second_ref, out_ref, send_ref
):
    tile = pl.program_id(0)
    first, second, mine = flags[0], flags[1], flags[2]
    tile_first, tile_second = first_ref[...], second_ref[...]
    product = outer(tile_first, own_first_ref[...]) + outer(tile_second, own_second_ref[...])
    dead_row = (tile == first) | (tile == second)
    updated = jnp.where(dead_row, 0.0, front_ref[...] - product)
    out_ref[...] = jnp.where(
        mine == first, tile_first, jnp.where(mine == second, tile_second, updated)
    )
    dead_column = (mine == first) | (mine == second)
    send_ref[0] = jnp.where(dead_column, 0.0, updated)


def update(front, panel_first, panel_second, flags, place):
    rows, size = front.shape
    count = rows // size
    mine = lambda i, flags, place: (i, 0)
    own = lambda i, flags, place: (flags[2], 0)
    block = (size, size)
    return pl.pallas_call(
        update_kernel,
        grid_spec=pltpu.PrefetchScalarGridSpec(
            num_scalar_prefetch=2,
            grid=(count,),
            in_specs=[pl.BlockSpec(block, mine)] * 3 + [pl.BlockSpec(block, own)] * 2,
            out_specs=[
                pl.BlockSpec(block, mine),
                pl.BlockSpec((1, size, size), lambda i, flags, place: (place[i], 0, 0)),
            ],
        ),
        out_shape=(
            jax.ShapeDtypeStruct((rows, size), jnp.float32),
            jax.ShapeDtypeStruct((count, size, size), jnp.float32),
        ),
        name="update",
    )(flags, place, front, panel_first, panel_second, panel_first, panel_second)


def place_kernel(source, tile_ref, out_ref):
    out_ref[...] = tile_ref[0]


def place_tiles(tiles, inverse):
    count, size, _ = tiles.shape
    return pl.pallas_call(
        place_kernel,
        grid_spec=pltpu.PrefetchScalarGridSpec(
            num_scalar_prefetch=1,
            grid=(count,),
            in_specs=[pl.BlockSpec((1, size, size), lambda b, source: (source[b], 0, 0))],
            out_specs=pl.BlockSpec((size, size), lambda b, source: (0, b)),
        ),
        out_shape=jax.ShapeDtypeStruct((size, count * size), jnp.float32),
        name="place",
    )(inverse, tiles)


def block_row(tiles, pivot_block):
    return lax.dynamic_index_in_dim(tiles, pivot_block, 0, keepdims=False)


def shards(leaf_fronts, root_front, leaf_order, leaf_map, root_order):
    order_rows, block_size = leaf_fronts.shape
    block_count = order_rows // block_size
    my_block = lax.axis_index("front").astype(jnp.int32)
    leaf_index = lax.axis_index("leaf")
    slice_width = root_front.shape[2]
    block_ids = jnp.arange(block_count, dtype=jnp.int32)
    own_start = my_block * block_size

    tiles = leaf_fronts.reshape(block_count, block_size, block_size)
    first, second = leaf_order[0, 0], leaf_order[0, 1]
    raw_first = lax.all_gather(block_row(tiles, first).T, "front", axis=0, tiled=True)
    raw_second = lax.all_gather(block_row(tiles, second).T, "front", axis=0, tiled=True)
    everything = jnp.ones((block_count,), dtype=jnp.bool_)
    panel_first = make_panel(raw_first, first, everything)
    raw_second, root_rows = lax.optimization_barrier((raw_second, root_front[:, 0, :].T))
    pivot_rows = lax.dynamic_slice_in_dim(panel_first, second * block_size, block_size, 0)
    raw_second = raw_second - jnp.dot(panel_first, pivot_rows.T, precision=HIGH)
    panel_second = make_panel(raw_second, second, block_ids != first)

    flags = jnp.stack([first, second, my_block])
    leaf_out, outgoing = update(leaf_fronts, panel_first, panel_second, flags, leaf_map[0])
    incoming = lax.all_to_all(outgoing, "front", split_axis=0, concat_axis=0, tiled=True)
    gathered = place_tiles(incoming, invert(leaf_map[0]))
    part = lax.psum_scatter(gathered, "leaf", scatter_dimension=0, tiled=True)
    part = part + root_rows

    pivot = root_order[0]
    row = lax.dynamic_slice_in_dim(part, pivot * block_size, block_size, 1)
    row = lax.all_gather(row, "leaf", axis=0, tiled=True)
    raw_root = lax.all_gather(row, "front", axis=0, tiled=True)
    panel = make_panel(raw_root, pivot, everything)
    own = lax.dynamic_slice_in_dim(panel, own_start + leaf_index * slice_width, slice_width, 0)
    part = part - jnp.dot(own, panel.T, precision=HIGH)
    part = part.reshape(slice_width, block_count, block_size)
    part = jnp.where((block_ids != pivot)[None, :, None], part, 0.0)
    part = part.reshape(slice_width, order_rows)
    own_panel = lax.dynamic_slice_in_dim(panel, leaf_index * slice_width, slice_width, 1)
    root_out = jnp.where(my_block == pivot, own_panel, part.T)
    return (leaf_out, root_out[:, None, :])


def solution(mesh):
    return jax.shard_map(
        shards,
        mesh=mesh,
        in_specs=(
            P("leaf", "front"),
            P(None, "front", "leaf"),
            P("leaf", None),
            P("leaf", None),
            P(),
        ),
        out_specs=(P("leaf", "front"), P(None, "front", "leaf")),
        check_vma=False,
    )
```

```python
import jax
import jax.numpy as jnp
from jax import lax
from jax.experimental import pallas as pl
from jax.experimental.pallas import tpu as pltpu
from jax.sharding import PartitionSpec as P

HIGH = lax.Precision.HIGH
HIGHEST = lax.Precision.HIGHEST
STEP = 32
GROUP = 8
LANES = 128


def invert(permutation):
    block_ids = jnp.arange(permutation.shape[0], dtype=jnp.int32)
    hits = permutation[None, :] == block_ids[:, None]
    return jnp.sum(jnp.where(hits, block_ids[None, :], 0), axis=1).astype(jnp.int32)


def factor(diag, work_ref, upper_ref, inverse_ref):
    size = diag.shape[0]
    work_ref[:, :size] = diag
    rows = lax.broadcasted_iota(jnp.int32, (size, size), 0)
    lanes = lax.broadcasted_iota(jnp.int32, (size, size), 1)
    work_ref[:, size:] = jnp.where(rows == lanes, 1.0, 0.0)
    row_ids = lax.broadcasted_iota(jnp.int32, (STEP, LANES), 0)
    lane_ids = lax.broadcasted_iota(jnp.int32, (STEP, LANES), 1)
    for start in range(0, size, STEP):
        base = start // LANES * LANES
        tile = work_ref[start : start + STEP, base : base + LANES]
        unit = jnp.where(row_ids == lane_ids, 1.0, 0.0)
        roots = jnp.ones((STEP, LANES), jnp.float32)
        for group in range(0, STEP, GROUP):
            lane = start - base + group
            columns = [
                jnp.broadcast_to(tile[:, lane + k : lane + k + 1], (STEP, LANES))
                for k in range(GROUP)
            ]
            for k in range(GROUP):
                row = group + k
                pivot = columns[k][row : row + 1, :]
                roots = jnp.where(row_ids == row, pivot, roots)
                if row == STEP - 1:
                    break
                scaled = jnp.where(row_ids > row, columns[k] * (1.0 / pivot), 0.0)
                for later in range(k + 1, GROUP):
                    columns[later] = columns[later] - scaled * columns[later][row : row + 1, :]
                tile = tile - scaled * tile[row : row + 1, :]
                unit = unit - scaled * unit[row : row + 1, :]
        small = (unit / jnp.sqrt(roots))[:, :STEP]
        final = jnp.dot(
            small,
            work_ref[start : start + STEP, :],
            precision=HIGHEST,
            preferred_element_type=jnp.float32,
        )
        upper_ref[start : start + STEP, :] = final[:, :size]
        inverse_ref[start : start + STEP, :] = final[:, size:]
        if start + STEP < size:
            below = start + STEP
            update = lax.dot_general(
                final[:, below // LANES * LANES : size],
                final,
                (((0,), (0,)), ((), ())),
                precision=HIGHEST,
                preferred_element_type=jnp.float32,
            )
            skip = below - below // LANES * LANES
            work_ref[below:, :] = work_ref[below:, :] - update[skip:, :]
    lower = jnp.where(rows >= lanes, upper_ref[...].T, 0.0)
    inverse_t = jnp.where(rows <= lanes, inverse_ref[...].T, 0.0)
    return lower, inverse_t


def panel_kernel(pivot, keep, raw_ref, diag_ref, *rest):
    before, (out_ref, work_ref, lower_ref, inverse_ref, before_ref) = rest[:-5], rest[-5:]
    step = pl.program_id(0)

    @pl.when(step == 0)
    def _():
        diag = diag_ref[...]
        if before:
            pivot_rows = before[1][...]
            before_ref[...] = pivot_rows.T
            diag = diag - jnp.dot(
                pivot_rows,
                before_ref[...],
                precision=HIGHEST,
                preferred_element_type=jnp.float32,
            )
        lower, inverse_t = factor(diag, work_ref, lower_ref, inverse_ref)
        lower_ref[...] = lower
        inverse_ref[...] = inverse_t

    @pl.when(step > 0)
    def _():
        tile = step - 1
        raw = raw_ref[...]
        if before:
            raw = raw - product(before[0][...], before_ref[...])
        solved = jnp.dot(
            raw, inverse_ref[...], precision=HIGHEST, preferred_element_type=jnp.float32
        )
        solved = jnp.where(keep[tile] != 0, solved, 0.0)
        out_ref[...] = jnp.where(tile == pivot[0], lower_ref[...], solved)


def make_panel(raw_column, pivot_block, alive_set, before=None):
    rows, size = raw_column.shape
    count = rows // size
    block = (size, size)
    tile = pl.BlockSpec(block, lambda s, pivot, keep: (jnp.maximum(s - 1, 0), 0))
    fixed = pl.BlockSpec(block, lambda s, pivot, keep: (pivot[0], 0))
    extra = () if before is None else (before, before)
    return pl.pallas_call(
        panel_kernel,
        grid_spec=pltpu.PrefetchScalarGridSpec(
            num_scalar_prefetch=2,
            grid=(count + 1,),
            in_specs=[tile, fixed] * (2 if extra else 1),
            out_specs=tile,
            scratch_shapes=[
                pltpu.VMEM((size, 2 * size), jnp.float32),
                pltpu.VMEM(block, jnp.float32),
                pltpu.VMEM(block, jnp.float32),
                pltpu.VMEM(block, jnp.float32),
            ],
        ),
        out_shape=jax.ShapeDtypeStruct((rows, size), jnp.float32),
        name="panel",
    )(pivot_block[None], alive_set.astype(jnp.int32), raw_column, raw_column, *extra)


def halves(value):
    top = value.astype(jnp.bfloat16)
    return top, (value - top.astype(jnp.float32)).astype(jnp.bfloat16)


def product(left, right):
    return split_product(left, *halves(right))


def split_product(left, right_top, right_low):
    top, low = halves(left)
    dot = lambda a, b: jnp.dot(a, b, preferred_element_type=jnp.float32)
    return dot(top, right_top) + (dot(top, right_low) + dot(low, right_top))


def update_kernel(
    flags, place, front_ref, first_ref, second_ref, own_first_ref, own_second_ref,
    out_ref, send_ref, top_ref, low_ref,
):
    tile = pl.program_id(0)
    first, second, mine = flags[0], flags[1], flags[2]

    @pl.when(tile == 0)
    def _():
        for slot, own in enumerate((own_first_ref, own_second_ref)):
            top, low = halves(own[...].T)
            top_ref[slot] = top
            low_ref[slot] = low

    tile_first, tile_second = first_ref[...], second_ref[...]
    total = split_product(tile_first, top_ref[0], low_ref[0]) + split_product(
        tile_second, top_ref[1], low_ref[1]
    )
    dead_row = (tile == first) | (tile == second)
    updated = jnp.where(dead_row, 0.0, front_ref[...] - total)
    out_ref[...] = jnp.where(
        mine == first, tile_first, jnp.where(mine == second, tile_second, updated)
    )
    dead_column = (mine == first) | (mine == second)
    send_ref[0] = jnp.where(dead_column, 0.0, updated)


def update(front, panel_first, panel_second, flags, place):
    rows, size = front.shape
    count = rows // size
    mine = lambda i, flags, place: (i, 0)
    own = lambda i, flags, place: (flags[2], 0)
    block = (size, size)
    return pl.pallas_call(
        update_kernel,
        grid_spec=pltpu.PrefetchScalarGridSpec(
            num_scalar_prefetch=2,
            grid=(count,),
            in_specs=[pl.BlockSpec(block, mine)] * 3 + [pl.BlockSpec(block, own)] * 2,
            out_specs=[
                pl.BlockSpec(block, mine),
                pl.BlockSpec((1, size, size), lambda i, flags, place: (place[i], 0, 0)),
            ],
            scratch_shapes=[pltpu.VMEM((2, size, size), jnp.bfloat16)] * 2,
        ),
        out_shape=(
            jax.ShapeDtypeStruct((rows, size), jnp.float32),
            jax.ShapeDtypeStruct((count, size, size), jnp.float32),
        ),
        name="update",
    )(flags, place, front, panel_first, panel_second, panel_first, panel_second)


def place_kernel(source, tile_ref, out_ref):
    out_ref[...] = tile_ref[0]


def place_tiles(tiles, inverse):
    count, size, _ = tiles.shape
    return pl.pallas_call(
        place_kernel,
        grid_spec=pltpu.PrefetchScalarGridSpec(
            num_scalar_prefetch=1,
            grid=(count,),
            in_specs=[pl.BlockSpec((1, size, size), lambda b, source: (source[b], 0, 0))],
            out_specs=pl.BlockSpec((size, size), lambda b, source: (0, b)),
        ),
        out_shape=jax.ShapeDtypeStruct((size, count * size), jnp.float32),
        name="place",
    )(inverse, tiles)


def block_row(tiles, pivot_block):
    return lax.dynamic_index_in_dim(tiles, pivot_block, 0, keepdims=False)


def shards(leaf_fronts, root_front, leaf_order, leaf_map, root_order):
    order_rows, block_size = leaf_fronts.shape
    block_count = order_rows // block_size
    my_block = lax.axis_index("front").astype(jnp.int32)
    leaf_index = lax.axis_index("leaf")
    slice_width = root_front.shape[2]
    block_ids = jnp.arange(block_count, dtype=jnp.int32)
    own_start = my_block * block_size

    tiles = leaf_fronts.reshape(block_count, block_size, block_size)
    first, second = leaf_order[0, 0], leaf_order[0, 1]
    raw_first = lax.all_gather(block_row(tiles, first).T, "front", axis=0, tiled=True)
    raw_second = lax.all_gather(block_row(tiles, second).T, "front", axis=0, tiled=True)
    inverse = invert(leaf_map[0])
    pivot = root_order[0]
    source = inverse[pivot]
    raw_source = lax.all_gather(block_row(tiles, source).T, "front", axis=0, tiled=True)
    everything = jnp.ones((block_count,), dtype=jnp.bool_)
    panel_first = make_panel(raw_first, first, everything)
    root_rows = root_front[:, 0, :].T
    raw_second, raw_source, root_rows = lax.optimization_barrier(
        (raw_second, raw_source, root_rows)
    )
    panel_second = make_panel(raw_second, second, block_ids != first, panel_first)

    into = inverse[my_block]
    rows_of = lambda panel, block: lax.dynamic_slice_in_dim(
        panel, block * block_size, block_size, 0
    )
    share = rows_of(raw_source, into)
    for panel in (panel_first, panel_second):
        share = share - jnp.dot(rows_of(panel, into), rows_of(panel, source).T, precision=HIGH)
    live = (into != first) & (into != second) & (source != first) & (source != second)
    share = jnp.where(live, share, 0.0)
    root_share = lax.dynamic_slice_in_dim(root_rows, pivot * block_size, block_size, 1)
    here = leaf_index * slice_width
    widened = jnp.zeros_like(share)
    widened = lax.dynamic_update_slice_in_dim(widened, root_share, here, 0)
    raw_root = lax.psum(share + widened, "leaf")
    raw_root = lax.all_gather(raw_root, "front", axis=0, tiled=True)

    flags = jnp.stack([first, second, my_block])
    leaf_out, outgoing = update(leaf_fronts, panel_first, panel_second, flags, leaf_map[0])
    incoming = lax.all_to_all(outgoing, "front", split_axis=0, concat_axis=0, tiled=True)
    gathered = place_tiles(incoming, inverse)
    part = lax.psum_scatter(gathered, "leaf", scatter_dimension=0, tiled=True)
    part = part + root_rows

    panel = make_panel(raw_root, pivot, everything)
    own = lax.dynamic_slice_in_dim(panel, own_start + leaf_index * slice_width, slice_width, 0)
    part = part - jnp.dot(own, panel.T, precision=HIGH)
    part = part.reshape(slice_width, block_count, block_size)
    part = jnp.where((block_ids != pivot)[None, :, None], part, 0.0)
    part = part.reshape(slice_width, order_rows)
    own_panel = lax.dynamic_slice_in_dim(panel, leaf_index * slice_width, slice_width, 1)
    root_out = jnp.where(my_block == pivot, own_panel, part.T)
    return (leaf_out, root_out[:, None, :])


def solution(mesh):
    return jax.shard_map(
        shards,
        mesh=mesh,
        in_specs=(
            P("leaf", "front"),
            P(None, "front", "leaf"),
            P("leaf", None),
            P("leaf", None),
            P(),
        ),
        out_specs=(P("leaf", "front"), P(None, "front", "leaf")),
        check_vma=False,
    )
```

```python
import jax
import jax.numpy as jnp
from jax import lax
from jax.experimental import pallas as pl
from jax.experimental.pallas import tpu as pltpu
from jax.sharding import PartitionSpec as P

HIGH = lax.Precision.HIGH
HIGHEST = lax.Precision.HIGHEST
STEP = 32
GROUP = 8
LANES = 128


def invert(permutation):
    block_ids = jnp.arange(permutation.shape[0], dtype=jnp.int32)
    hits = permutation[None, :] == block_ids[:, None]
    return jnp.sum(jnp.where(hits, block_ids[None, :], 0), axis=1).astype(jnp.int32)


def factor(diag, work_ref, upper_ref, inverse_ref):
    size = diag.shape[0]
    work_ref[:, :size] = diag
    rows = lax.broadcasted_iota(jnp.int32, (size, size), 0)
    lanes = lax.broadcasted_iota(jnp.int32, (size, size), 1)
    work_ref[:, size:] = jnp.where(rows == lanes, 1.0, 0.0)
    row_ids = lax.broadcasted_iota(jnp.int32, (STEP, LANES), 0)
    lane_ids = lax.broadcasted_iota(jnp.int32, (STEP, LANES), 1)
    for start in range(0, size, STEP):
        base = start // LANES * LANES
        tile = work_ref[start : start + STEP, base : base + LANES]
        unit = jnp.where(row_ids == lane_ids, 1.0, 0.0)
        roots = jnp.ones((STEP, LANES), jnp.float32)
        for group in range(0, STEP, GROUP):
            lane = start - base + group
            columns = [
                jnp.broadcast_to(tile[:, lane + k : lane + k + 1], (STEP, LANES))
                for k in range(GROUP)
            ]
            for k in range(GROUP):
                row = group + k
                pivot = columns[k][row : row + 1, :]
                roots = jnp.where(row_ids == row, pivot, roots)
                if row == STEP - 1:
                    break
                scaled = jnp.where(row_ids > row, columns[k] * (1.0 / pivot), 0.0)
                for later in range(k + 1, GROUP):
                    columns[later] = columns[later] - scaled * columns[later][row : row + 1, :]
                tile = tile - scaled * tile[row : row + 1, :]
                unit = unit - scaled * unit[row : row + 1, :]
        small = (unit / jnp.sqrt(roots))[:, :STEP]
        final = jnp.dot(
            small,
            work_ref[start : start + STEP, :],
            precision=HIGHEST,
            preferred_element_type=jnp.float32,
        )
        upper_ref[start : start + STEP, :] = final[:, :size]
        inverse_ref[start : start + STEP, :] = final[:, size:]
        if start + STEP < size:
            below = start + STEP
            update = lax.dot_general(
                final[:, below // LANES * LANES : size],
                final,
                (((0,), (0,)), ((), ())),
                precision=HIGHEST,
                preferred_element_type=jnp.float32,
            )
            skip = below - below // LANES * LANES
            work_ref[below:, :] = work_ref[below:, :] - update[skip:, :]
    lower = jnp.where(rows >= lanes, upper_ref[...].T, 0.0)
    inverse_t = jnp.where(rows <= lanes, inverse_ref[...].T, 0.0)
    return lower, inverse_t


def panel_kernel(pivot, keep, raw_ref, diag_ref, *rest):
    before, (out_ref, work_ref, lower_ref, inverse_ref, before_ref) = rest[:-5], rest[-5:]
    step = pl.program_id(0)

    @pl.when(step == 0)
    def _():
        diag = diag_ref[...]
        if before:
            pivot_rows = before[1][...]
            before_ref[...] = pivot_rows.T
            diag = diag - jnp.dot(
                pivot_rows,
                before_ref[...],
                precision=HIGHEST,
                preferred_element_type=jnp.float32,
            )
        lower, inverse_t = factor(diag, work_ref, lower_ref, inverse_ref)
        lower_ref[...] = lower
        inverse_ref[...] = inverse_t

    @pl.when(step > 0)
    def _():
        tile = step - 1
        raw = raw_ref[...]
        if before:
            raw = raw - product(before[0][...], before_ref[...])
        solved = jnp.dot(
            raw, inverse_ref[...], precision=HIGHEST, preferred_element_type=jnp.float32
        )
        solved = jnp.where(keep[tile] != 0, solved, 0.0)
        out_ref[...] = jnp.where(tile == pivot[0], lower_ref[...], solved)


def make_panel(raw_column, pivot_block, alive_set, before=None):
    rows, size = raw_column.shape
    count = rows // size
    block = (size, size)
    tile = pl.BlockSpec(block, lambda s, pivot, keep: (jnp.maximum(s - 1, 0), 0))
    fixed = pl.BlockSpec(block, lambda s, pivot, keep: (pivot[0], 0))
    extra = () if before is None else (before, before)
    return pl.pallas_call(
        panel_kernel,
        grid_spec=pltpu.PrefetchScalarGridSpec(
            num_scalar_prefetch=2,
            grid=(count + 1,),
            in_specs=[tile, fixed] * (2 if extra else 1),
            out_specs=tile,
            scratch_shapes=[
                pltpu.VMEM((size, 2 * size), jnp.float32),
                pltpu.VMEM(block, jnp.float32),
                pltpu.VMEM(block, jnp.float32),
                pltpu.VMEM(block, jnp.float32),
            ],
        ),
        out_shape=jax.ShapeDtypeStruct((rows, size), jnp.float32),
        name="panel",
        cost_estimate=pl.CostEstimate(
            flops=24 * rows * size * size, bytes_accessed=64 * rows * size, transcendentals=0
        ),
    )(pivot_block[None], alive_set.astype(jnp.int32), raw_column, raw_column, *extra)


def halves(value):
    top = value.astype(jnp.bfloat16)
    return top, (value - top.astype(jnp.float32)).astype(jnp.bfloat16)


def product(left, right):
    return split_product(left, *halves(right))


def split_product(left, right_top, right_low):
    top, low = halves(left)
    dot = lambda a, b: jnp.dot(a, b, preferred_element_type=jnp.float32)
    return dot(top, right_top) + (dot(top, right_low) + dot(low, right_top))


def update_kernel(
    flags, place, front_ref, first_ref, second_ref, own_first_ref, own_second_ref,
    out_ref, send_ref, top_ref, low_ref,
):
    tile = pl.program_id(0)
    first, second, mine = flags[0], flags[1], flags[2]

    @pl.when(tile == 0)
    def _():
        for slot, own in enumerate((own_first_ref, own_second_ref)):
            top, low = halves(own[...].T)
            top_ref[slot] = top
            low_ref[slot] = low

    tile_first, tile_second = first_ref[...], second_ref[...]
    total = split_product(tile_first, top_ref[0], low_ref[0]) + split_product(
        tile_second, top_ref[1], low_ref[1]
    )
    dead_row = (tile == first) | (tile == second)
    updated = jnp.where(dead_row, 0.0, front_ref[...] - total)
    out_ref[...] = jnp.where(
        mine == first, tile_first, jnp.where(mine == second, tile_second, updated)
    )
    dead_column = (mine == first) | (mine == second)
    send_ref[0] = jnp.where(dead_column, 0.0, updated)


def update(front, panel_first, panel_second, flags, place):
    rows, size = front.shape
    count = rows // size
    mine = lambda i, flags, place: (i, 0)
    own = lambda i, flags, place: (flags[2], 0)
    block = (size, size)
    return pl.pallas_call(
        update_kernel,
        grid_spec=pltpu.PrefetchScalarGridSpec(
            num_scalar_prefetch=2,
            grid=(count,),
            in_specs=[pl.BlockSpec(block, mine)] * 3 + [pl.BlockSpec(block, own)] * 2,
            out_specs=[
                pl.BlockSpec(block, mine),
                pl.BlockSpec((1, size, size), lambda i, flags, place: (place[i], 0, 0)),
            ],
            scratch_shapes=[pltpu.VMEM((2, size, size), jnp.bfloat16)] * 2,
        ),
        out_shape=(
            jax.ShapeDtypeStruct((rows, size), jnp.float32),
            jax.ShapeDtypeStruct((count, size, size), jnp.float32),
        ),
        name="update",
        cost_estimate=pl.CostEstimate(
            flops=12 * rows * size * size, bytes_accessed=32 * rows * size, transcendentals=0
        ),
    )(flags, place, front, panel_first, panel_second, panel_first, panel_second)


def place_kernel(source, tile_ref, out_ref):
    out_ref[...] = tile_ref[0]


def place_tiles(tiles, inverse):
    count, size, _ = tiles.shape
    return pl.pallas_call(
        place_kernel,
        grid_spec=pltpu.PrefetchScalarGridSpec(
            num_scalar_prefetch=1,
            grid=(count,),
            in_specs=[pl.BlockSpec((1, size, size), lambda b, source: (source[b], 0, 0))],
            out_specs=pl.BlockSpec((size, size), lambda b, source: (0, b)),
        ),
        out_shape=jax.ShapeDtypeStruct((size, count * size), jnp.float32),
        name="place",
    )(inverse, tiles)


def block_row(tiles, pivot_block):
    return lax.dynamic_index_in_dim(tiles, pivot_block, 0, keepdims=False)


def shards(leaf_fronts, root_front, leaf_order, leaf_map, root_order):
    order_rows, block_size = leaf_fronts.shape
    block_count = order_rows // block_size
    my_block = lax.axis_index("front").astype(jnp.int32)
    leaf_index = lax.axis_index("leaf")
    slice_width = root_front.shape[2]
    block_ids = jnp.arange(block_count, dtype=jnp.int32)
    own_start = my_block * block_size

    tiles = leaf_fronts.reshape(block_count, block_size, block_size)
    first, second = leaf_order[0, 0], leaf_order[0, 1]
    inverse = invert(leaf_map[0])
    pivot = root_order[0]
    source = inverse[pivot]
    row_first = block_row(tiles, first).T
    row_second = block_row(tiles, second).T
    row_source = block_row(tiles, source).T
    raw_first = lax.all_gather(row_first, "front", axis=0, tiled=True)
    raw_first, row_second = lax.optimization_barrier((raw_first, row_second))
    raw_second = lax.all_gather(row_second, "front", axis=0, tiled=True)
    everything = jnp.ones((block_count,), dtype=jnp.bool_)
    panel_first = make_panel(raw_first, first, everything)
    root_rows = root_front[:, 0, :].T
    raw_second, root_rows, row_source, panel_first = lax.optimization_barrier(
        (raw_second, root_rows, row_source, panel_first)
    )
    raw_source = lax.all_gather(row_source, "front", axis=0, tiled=True)
    panel_second = make_panel(raw_second, second, block_ids != first, panel_first)

    flags = jnp.stack([first, second, my_block])
    leaf_out, outgoing = update(leaf_fronts, panel_first, panel_second, flags, leaf_map[0])
    raw_source, outgoing = lax.optimization_barrier((raw_source, outgoing))

    into = inverse[my_block]
    rows_of = lambda panel, block: lax.dynamic_slice_in_dim(
        panel, block * block_size, block_size, 0
    )
    share = rows_of(raw_source, into)
    for panel in (panel_first, panel_second):
        share = share - jnp.dot(rows_of(panel, into), rows_of(panel, source).T, precision=HIGH)
    live = (into != first) & (into != second) & (source != first) & (source != second)
    share = jnp.where(live, share, 0.0)
    root_share = lax.dynamic_slice_in_dim(root_rows, pivot * block_size, block_size, 1)
    here = leaf_index * slice_width
    widened = jnp.zeros_like(share)
    widened = lax.dynamic_update_slice_in_dim(widened, root_share, here, 0)
    shares = lax.all_gather(share + widened, "leaf", axis=0)
    raw_root = jnp.sum(shares, axis=0)
    raw_root = lax.all_gather(raw_root, "front", axis=0, tiled=True)

    incoming = lax.all_to_all(outgoing, "front", split_axis=0, concat_axis=0, tiled=True)
    gathered = place_tiles(incoming, inverse)
    gathered, raw_root = lax.optimization_barrier((gathered, raw_root))
    part = lax.psum_scatter(gathered, "leaf", scatter_dimension=0, tiled=True)
    part = part + root_rows

    panel = make_panel(raw_root, pivot, everything)
    own = lax.dynamic_slice_in_dim(panel, own_start + leaf_index * slice_width, slice_width, 0)
    part = part - jnp.dot(own, panel.T, precision=HIGH)
    part = part.reshape(slice_width, block_count, block_size)
    part = jnp.where((block_ids != pivot)[None, :, None], part, 0.0)
    part = part.reshape(slice_width, order_rows)
    own_panel = lax.dynamic_slice_in_dim(panel, leaf_index * slice_width, slice_width, 1)
    root_out = jnp.where(my_block == pivot, own_panel, part.T)
    return (leaf_out, root_out[:, None, :])


def solution(mesh):
    return jax.shard_map(
        shards,
        mesh=mesh,
        in_specs=(
            P("leaf", "front"),
            P(None, "front", "leaf"),
            P("leaf", None),
            P("leaf", None),
            P(),
        ),
        out_specs=(P("leaf", "front"), P(None, "front", "leaf")),
        check_vma=False,
    )
```

```python
import jax
import jax.numpy as jnp
from jax import lax
from jax.experimental import pallas as pl
from jax.experimental.pallas import tpu as pltpu
from jax.sharding import PartitionSpec as P

HIGH = lax.Precision.HIGH
HIGHEST = lax.Precision.HIGHEST
STEP = 32
GROUP = 8
LANES = 128


def invert(permutation):
    block_ids = jnp.arange(permutation.shape[0], dtype=jnp.int32)
    hits = permutation[None, :] == block_ids[:, None]
    return jnp.sum(jnp.where(hits, block_ids[None, :], 0), axis=1).astype(jnp.int32)


def factor(diag, work_ref, upper_ref, inverse_ref):
    size = diag.shape[0]
    work_ref[:, :size] = diag
    rows = lax.broadcasted_iota(jnp.int32, (size, size), 0)
    lanes = lax.broadcasted_iota(jnp.int32, (size, size), 1)
    work_ref[:, size:] = jnp.where(rows == lanes, 1.0, 0.0)
    row_ids = lax.broadcasted_iota(jnp.int32, (STEP, LANES), 0)
    lane_ids = lax.broadcasted_iota(jnp.int32, (STEP, LANES), 1)
    for start in range(0, size, STEP):
        base = start // LANES * LANES
        tile = work_ref[start : start + STEP, base : base + LANES]
        unit = jnp.where(row_ids == lane_ids, 1.0, 0.0)
        roots = jnp.ones((STEP, LANES), jnp.float32)
        for group in range(0, STEP, GROUP):
            lane = start - base + group
            columns = [
                jnp.broadcast_to(tile[:, lane + k : lane + k + 1], (STEP, LANES))
                for k in range(GROUP)
            ]
            for k in range(GROUP):
                row = group + k
                pivot = columns[k][row : row + 1, :]
                roots = jnp.where(row_ids == row, pivot, roots)
                if row == STEP - 1:
                    break
                scaled = jnp.where(row_ids > row, columns[k] * (1.0 / pivot), 0.0)
                for later in range(k + 1, GROUP):
                    columns[later] = columns[later] - scaled * columns[later][row : row + 1, :]
                tile = tile - scaled * tile[row : row + 1, :]
                unit = unit - scaled * unit[row : row + 1, :]
        small = (unit / jnp.sqrt(roots))[:, :STEP]
        final = jnp.dot(
            small,
            work_ref[start : start + STEP, :],
            precision=HIGHEST,
            preferred_element_type=jnp.float32,
        )
        upper_ref[start : start + STEP, :] = final[:, :size]
        inverse_ref[start : start + STEP, :] = final[:, size:]
        if start + STEP < size:
            below = start + STEP
            update = lax.dot_general(
                final[:, below // LANES * LANES : size],
                final,
                (((0,), (0,)), ((), ())),
                precision=HIGHEST,
                preferred_element_type=jnp.float32,
            )
            skip = below - below // LANES * LANES
            work_ref[below:, :] = work_ref[below:, :] - update[skip:, :]
    lower = jnp.where(rows >= lanes, upper_ref[...].T, 0.0)
    inverse_t = jnp.where(rows <= lanes, inverse_ref[...].T, 0.0)
    return lower, inverse_t


def panel_kernel(pivot, keep, raw_ref, diag_ref, *rest):
    before, (out_ref, work_ref, lower_ref, inverse_ref, before_ref) = rest[:-5], rest[-5:]
    step = pl.program_id(0)

    @pl.when(step == 0)
    def _():
        diag = diag_ref[...]
        if before:
            pivot_rows = before[1][...]
            before_ref[...] = pivot_rows.T
            diag = diag - jnp.dot(
                pivot_rows,
                before_ref[...],
                precision=HIGHEST,
                preferred_element_type=jnp.float32,
            )
        lower, inverse_t = factor(diag, work_ref, lower_ref, inverse_ref)
        lower_ref[...] = lower
        inverse_ref[...] = inverse_t

    @pl.when(step > 0)
    def _():
        tile = step - 1
        raw = raw_ref[...]
        if before:
            raw = raw - product(before[0][...], before_ref[...])
        solved = jnp.dot(
            raw, inverse_ref[...], precision=HIGHEST, preferred_element_type=jnp.float32
        )
        solved = jnp.where(keep[tile] != 0, solved, 0.0)
        out_ref[...] = jnp.where(tile == pivot[0], lower_ref[...], solved)


def make_panel(raw_column, pivot_block, alive_set, before=None):
    rows, size = raw_column.shape
    count = rows // size
    block = (size, size)
    tile = pl.BlockSpec(block, lambda s, pivot, keep: (jnp.maximum(s - 1, 0), 0))
    fixed = pl.BlockSpec(block, lambda s, pivot, keep: (pivot[0], 0))
    extra = () if before is None else (before, before)
    return pl.pallas_call(
        panel_kernel,
        grid_spec=pltpu.PrefetchScalarGridSpec(
            num_scalar_prefetch=2,
            grid=(count + 1,),
            in_specs=[tile, fixed] * (2 if extra else 1),
            out_specs=tile,
            scratch_shapes=[
                pltpu.VMEM((size, 2 * size), jnp.float32),
                pltpu.VMEM(block, jnp.float32),
                pltpu.VMEM(block, jnp.float32),
                pltpu.VMEM(block, jnp.float32),
            ],
        ),
        out_shape=jax.ShapeDtypeStruct((rows, size), jnp.float32),
        name="panel",
        cost_estimate=pl.CostEstimate(
            flops=24 * rows * size * size, bytes_accessed=64 * rows * size, transcendentals=0
        ),
    )(pivot_block[None], alive_set.astype(jnp.int32), raw_column, raw_column, *extra)


def halves(value):
    top = value.astype(jnp.bfloat16)
    return top, (value - top.astype(jnp.float32)).astype(jnp.bfloat16)


def product(left, right):
    return split_product(left, *halves(right))


def split_product(left, right_top, right_low):
    top, low = halves(left)
    dot = lambda a, b: jnp.dot(a, b, preferred_element_type=jnp.float32)
    return dot(top, right_top) + (dot(top, right_low) + dot(low, right_top))


def update_kernel(
    flags, place, front_ref, first_ref, second_ref, own_first_ref, own_second_ref,
    out_ref, send_ref, top_ref, low_ref,
):
    tile = pl.program_id(0)
    first, second, mine = flags[0], flags[1], flags[2]

    @pl.when(tile == 0)
    def _():
        for slot, own in enumerate((own_first_ref, own_second_ref)):
            top, low = halves(own[...].T)
            top_ref[slot] = top
            low_ref[slot] = low

    tile_first, tile_second = first_ref[...], second_ref[...]
    total = split_product(tile_first, top_ref[0], low_ref[0]) + split_product(
        tile_second, top_ref[1], low_ref[1]
    )
    dead_row = (tile == first) | (tile == second)
    updated = jnp.where(dead_row, 0.0, front_ref[...] - total)
    out_ref[...] = jnp.where(
        mine == first, tile_first, jnp.where(mine == second, tile_second, updated)
    )
    dead_column = (mine == first) | (mine == second)
    send_ref[0] = jnp.where(dead_column, 0.0, updated)


def update(front, panel_first, panel_second, flags, place):
    rows, size = front.shape
    count = rows // size
    mine = lambda i, flags, place: (i, 0)
    own = lambda i, flags, place: (flags[2], 0)
    block = (size, size)
    return pl.pallas_call(
        update_kernel,
        grid_spec=pltpu.PrefetchScalarGridSpec(
            num_scalar_prefetch=2,
            grid=(count,),
            in_specs=[pl.BlockSpec(block, mine)] * 3 + [pl.BlockSpec(block, own)] * 2,
            out_specs=[
                pl.BlockSpec(block, mine),
                pl.BlockSpec((1, size, size), lambda i, flags, place: (place[i], 0, 0)),
            ],
            scratch_shapes=[pltpu.VMEM((2, size, size), jnp.bfloat16)] * 2,
        ),
        out_shape=(
            jax.ShapeDtypeStruct((rows, size), jnp.float32),
            jax.ShapeDtypeStruct((count, size, size), jnp.float32),
        ),
        name="update",
        cost_estimate=pl.CostEstimate(
            flops=12 * rows * size * size, bytes_accessed=32 * rows * size, transcendentals=0
        ),
    )(flags, place, front, panel_first, panel_second, panel_first, panel_second)


def place_kernel(source, tile_ref, out_ref):
    out_ref[...] = tile_ref[0]


def place_tiles(tiles, inverse):
    count, size, _ = tiles.shape
    return pl.pallas_call(
        place_kernel,
        grid_spec=pltpu.PrefetchScalarGridSpec(
            num_scalar_prefetch=1,
            grid=(count,),
            in_specs=[pl.BlockSpec((1, size, size), lambda b, source: (source[b], 0, 0))],
            out_specs=pl.BlockSpec((size, size), lambda b, source: (0, b)),
        ),
        out_shape=jax.ShapeDtypeStruct((size, count * size), jnp.float32),
        name="place",
    )(inverse, tiles)


def finish_kernel(flags, part_ref, root_ref, panel_ref, own_ref, out_ref, turned_ref):
    width, columns = out_ref.shape
    size = panel_ref.shape[1]
    turned_ref[...] = panel_ref[...].T
    change = product(own_ref[...], turned_ref[...])
    mine = turned_ref[pl.ds(pl.multiple_of(flags[2] * width, width), width), :]
    first = flags[0] * size - pl.program_id(0) * columns
    lanes = lax.broadcasted_iota(jnp.int32, (width, columns), 1)
    dead = (lanes >= first) & (lanes < first + size)
    part = jnp.where(dead, 0.0, part_ref[...] + root_ref[...] - change)
    out_ref[...] = jnp.where(flags[0] == flags[1], mine, part)


def finish(part, root_rows, panel, flags):
    width, rows = part.shape
    size = panel.shape[1]
    chunk = 4 * size
    across = pl.BlockSpec((width, chunk), lambda b, flags: (0, b))
    return pl.pallas_call(
        finish_kernel,
        grid_spec=pltpu.PrefetchScalarGridSpec(
            num_scalar_prefetch=1,
            grid=(rows // chunk,),
            in_specs=[
                across,
                across,
                pl.BlockSpec((chunk, size), lambda b, flags: (b, 0)),
                pl.BlockSpec((width, size), lambda b, flags: (flags[3], 0)),
            ],
            out_specs=across,
            scratch_shapes=[pltpu.VMEM((size, chunk), jnp.float32)],
        ),
        out_shape=jax.ShapeDtypeStruct((width, rows), jnp.float32),
        name="finish",
    )(flags, part, root_rows, panel, panel)


def block_row(tiles, pivot_block):
    return lax.dynamic_index_in_dim(tiles, pivot_block, 0, keepdims=False)


def shards(leaf_fronts, root_front, leaf_order, leaf_map, root_order):
    order_rows, block_size = leaf_fronts.shape
    block_count = order_rows // block_size
    my_block = lax.axis_index("front").astype(jnp.int32)
    leaf_index = lax.axis_index("leaf").astype(jnp.int32)
    slice_width = root_front.shape[2]
    block_ids = jnp.arange(block_count, dtype=jnp.int32)

    tiles = leaf_fronts.reshape(block_count, block_size, block_size)
    first, second = leaf_order[0, 0], leaf_order[0, 1]
    inverse = invert(leaf_map[0])
    pivot = root_order[0]
    source = inverse[pivot]
    row_first = block_row(tiles, first).T
    row_second = block_row(tiles, second).T
    row_source = block_row(tiles, source).T
    raw_first = lax.all_gather(row_first, "front", axis=0, tiled=True)
    raw_first, row_second = lax.optimization_barrier((raw_first, row_second))
    raw_second = lax.all_gather(row_second, "front", axis=0, tiled=True)
    everything = jnp.ones((block_count,), dtype=jnp.bool_)
    panel_first = make_panel(raw_first, first, everything)
    root_rows = root_front[:, 0, :].T
    raw_second, root_rows, row_source, panel_first = lax.optimization_barrier(
        (raw_second, root_rows, row_source, panel_first)
    )
    raw_source = lax.all_gather(row_source, "front", axis=0, tiled=True)
    panel_second = make_panel(raw_second, second, block_ids != first, panel_first)

    flags = jnp.stack([first, second, my_block])
    leaf_out, outgoing = update(leaf_fronts, panel_first, panel_second, flags, leaf_map[0])
    raw_source, outgoing = lax.optimization_barrier((raw_source, outgoing))

    into = inverse[my_block]
    rows_of = lambda panel, block: lax.dynamic_slice_in_dim(
        panel, block * block_size, block_size, 0
    )
    share = rows_of(raw_source, into)
    for panel in (panel_first, panel_second):
        share = share - jnp.dot(rows_of(panel, into), rows_of(panel, source).T, precision=HIGH)
    live = (into != first) & (into != second) & (source != first) & (source != second)
    share = jnp.where(live, share, 0.0)
    root_share = lax.dynamic_slice_in_dim(root_rows, pivot * block_size, block_size, 1)
    here = leaf_index * slice_width
    widened = jnp.zeros_like(share)
    widened = lax.dynamic_update_slice_in_dim(widened, root_share, here, 0)
    shares = lax.all_gather(share + widened, "leaf", axis=0)
    incoming = lax.all_to_all(outgoing, "front", split_axis=0, concat_axis=0, tiled=True)
    shares, incoming = lax.optimization_barrier((shares, incoming))
    raw_root = jnp.sum(shares, axis=0)
    raw_root = lax.all_gather(raw_root, "front", axis=0, tiled=True)
    gathered = place_tiles(incoming, inverse)
    gathered, raw_root = lax.optimization_barrier((gathered, raw_root))
    part = lax.psum_scatter(gathered, "leaf", scatter_dimension=0, tiled=True)

    panel = make_panel(raw_root, pivot, everything)
    own_rows = my_block * (block_size // slice_width) + leaf_index
    ends = jnp.stack([pivot, my_block, leaf_index, own_rows])
    root_out = finish(part, root_rows, panel, ends).T
    return (leaf_out, root_out[:, None, :])


def solution(mesh):
    return jax.shard_map(
        shards,
        mesh=mesh,
        in_specs=(
            P("leaf", "front"),
            P(None, "front", "leaf"),
            P("leaf", None),
            P("leaf", None),
            P(),
        ),
        out_specs=(P("leaf", "front"), P(None, "front", "leaf")),
        check_vma=False,
    )
```

```python
import jax
import jax.numpy as jnp
from jax import lax
from jax.experimental import pallas as pl
from jax.experimental.pallas import tpu as pltpu
from jax.sharding import PartitionSpec as P

HIGH = lax.Precision.HIGH
HIGHEST = lax.Precision.HIGHEST
STEP = 32
GROUP = 8
LANES = 128


def invert(permutation):
    block_ids = jnp.arange(permutation.shape[0], dtype=jnp.int32)
    hits = permutation[None, :] == block_ids[:, None]
    return jnp.sum(jnp.where(hits, block_ids[None, :], 0), axis=1).astype(jnp.int32)


def factor(diag, work_ref, upper_ref, inverse_ref):
    size = diag.shape[0]
    work_ref[:, :size] = diag
    rows = lax.broadcasted_iota(jnp.int32, (size, size), 0)
    lanes = lax.broadcasted_iota(jnp.int32, (size, size), 1)
    work_ref[:, size:] = jnp.where(rows == lanes, 1.0, 0.0)
    row_ids = lax.broadcasted_iota(jnp.int32, (STEP, LANES), 0)
    lane_ids = lax.broadcasted_iota(jnp.int32, (STEP, LANES), 1)
    for start in range(0, size, STEP):
        base = start // LANES * LANES
        tile = work_ref[start : start + STEP, base : base + LANES]
        unit = jnp.where(row_ids == lane_ids, 1.0, 0.0)
        roots = jnp.ones((STEP, LANES), jnp.float32)
        for group in range(0, STEP, GROUP):
            lane = start - base + group
            columns = [
                jnp.broadcast_to(tile[:, lane + k : lane + k + 1], (STEP, LANES))
                for k in range(GROUP)
            ]
            for k in range(GROUP):
                row = group + k
                pivot = columns[k][row : row + 1, :]
                roots = jnp.where(row_ids == row, pivot, roots)
                if row == STEP - 1:
                    break
                scaled = jnp.where(row_ids > row, columns[k] * (1.0 / pivot), 0.0)
                for later in range(k + 1, GROUP):
                    columns[later] = columns[later] - scaled * columns[later][row : row + 1, :]
                tile = tile - scaled * tile[row : row + 1, :]
                unit = unit - scaled * unit[row : row + 1, :]
        small = (unit / jnp.sqrt(roots))[:, :STEP]
        final = jnp.dot(
            small,
            work_ref[start : start + STEP, :],
            precision=HIGHEST,
            preferred_element_type=jnp.float32,
        )
        upper_ref[start : start + STEP, :] = final[:, :size]
        inverse_ref[start : start + STEP, :] = final[:, size:]
        if start + STEP < size:
            below = start + STEP
            update = lax.dot_general(
                final[:, below // LANES * LANES : size],
                final,
                (((0,), (0,)), ((), ())),
                precision=HIGHEST,
                preferred_element_type=jnp.float32,
            )
            skip = below - below // LANES * LANES
            work_ref[below:, :] = work_ref[below:, :] - update[skip:, :]
    lower = jnp.where(rows >= lanes, upper_ref[...].T, 0.0)
    inverse_t = jnp.where(rows <= lanes, inverse_ref[...].T, 0.0)
    return lower, inverse_t


def panel_kernel(pivot, keep, raw_ref, diag_ref, *rest):
    before, (out_ref, work_ref, lower_ref, inverse_ref, before_ref) = rest[:-5], rest[-5:]
    step = pl.program_id(0)

    @pl.when(step == 0)
    def _():
        diag = diag_ref[...]
        if before:
            pivot_rows = before[1][...]
            before_ref[...] = pivot_rows.T
            diag = diag - jnp.dot(
                pivot_rows,
                before_ref[...],
                precision=HIGHEST,
                preferred_element_type=jnp.float32,
            )
        lower, inverse_t = factor(diag, work_ref, lower_ref, inverse_ref)
        lower_ref[...] = lower
        inverse_ref[...] = inverse_t

    @pl.when(step > 0)
    def _():
        tile = step - 1
        raw = raw_ref[...]
        if before:
            raw = raw - product(before[0][...], before_ref[...])
        solved = jnp.dot(
            raw, inverse_ref[...], precision=HIGHEST, preferred_element_type=jnp.float32
        )
        solved = jnp.where(keep[tile] != 0, solved, 0.0)
        out_ref[...] = jnp.where(tile == pivot[0], lower_ref[...], solved)


def make_panel(raw_column, pivot_block, alive_set, before=None):
    rows, size = raw_column.shape
    count = rows // size
    block = (size, size)
    tile = pl.BlockSpec(block, lambda s, pivot, keep: (jnp.maximum(s - 1, 0), 0))
    fixed = pl.BlockSpec(block, lambda s, pivot, keep: (pivot[0], 0))
    extra = () if before is None else (before, before)
    return pl.pallas_call(
        panel_kernel,
        grid_spec=pltpu.PrefetchScalarGridSpec(
            num_scalar_prefetch=2,
            grid=(count + 1,),
            in_specs=[tile, fixed] * (2 if extra else 1),
            out_specs=tile,
            scratch_shapes=[
                pltpu.VMEM((size, 2 * size), jnp.float32),
                pltpu.VMEM(block, jnp.float32),
                pltpu.VMEM(block, jnp.float32),
                pltpu.VMEM(block, jnp.float32),
            ],
        ),
        out_shape=jax.ShapeDtypeStruct((rows, size), jnp.float32),
        name="panel",
        cost_estimate=pl.CostEstimate(
            flops=24 * rows * size * size, bytes_accessed=64 * rows * size, transcendentals=0
        ),
    )(pivot_block[None], alive_set.astype(jnp.int32), raw_column, raw_column, *extra)


def halves(value):
    top = value.astype(jnp.bfloat16)
    return top, (value - top.astype(jnp.float32)).astype(jnp.bfloat16)


def product(left, right):
    return split_product(left, *halves(right))


def split_product(left, right_top, right_low):
    top, low = halves(left)
    dot = lambda a, b: jnp.dot(a, b, preferred_element_type=jnp.float32)
    return dot(top, right_top) + (dot(top, right_low) + dot(low, right_top))


def update_kernel(
    flags, place, front_ref, first_ref, second_ref, own_first_ref, own_second_ref,
    out_ref, send_ref, top_ref, low_ref,
):
    tile = pl.program_id(0)
    first, second, mine = flags[0], flags[1], flags[2]

    @pl.when(tile == 0)
    def _():
        for slot, own in enumerate((own_first_ref, own_second_ref)):
            top, low = halves(own[...].T)
            top_ref[slot] = top
            low_ref[slot] = low

    tile_first, tile_second = first_ref[...], second_ref[...]
    total = split_product(tile_first, top_ref[0], low_ref[0]) + split_product(
        tile_second, top_ref[1], low_ref[1]
    )
    dead_row = (tile == first) | (tile == second)
    updated = jnp.where(dead_row, 0.0, front_ref[...] - total)
    out_ref[...] = jnp.where(
        mine == first, tile_first, jnp.where(mine == second, tile_second, updated)
    )
    dead_column = (mine == first) | (mine == second)
    send_ref[0] = jnp.where(dead_column, 0.0, updated)


def update(front, panel_first, panel_second, flags, place):
    rows, size = front.shape
    count = rows // size
    mine = lambda i, flags, place: (i, 0)
    own = lambda i, flags, place: (flags[2], 0)
    block = (size, size)
    return pl.pallas_call(
        update_kernel,
        grid_spec=pltpu.PrefetchScalarGridSpec(
            num_scalar_prefetch=2,
            grid=(count,),
            in_specs=[pl.BlockSpec(block, mine)] * 3 + [pl.BlockSpec(block, own)] * 2,
            out_specs=[
                pl.BlockSpec(block, mine),
                pl.BlockSpec((1, size, size), lambda i, flags, place: (place[i], 0, 0)),
            ],
            scratch_shapes=[pltpu.VMEM((2, size, size), jnp.bfloat16)] * 2,
        ),
        out_shape=(
            jax.ShapeDtypeStruct((rows, size), jnp.float32),
            jax.ShapeDtypeStruct((count, size, size), jnp.float32),
        ),
        name="update",
        cost_estimate=pl.CostEstimate(
            flops=12 * rows * size * size, bytes_accessed=32 * rows * size, transcendentals=0
        ),
    )(flags, place, front, panel_first, panel_second, panel_first, panel_second)


def place_kernel(source, tile_ref, out_ref):
    out_ref[...] = tile_ref[0]


def place_tiles(tiles, inverse):
    count, size, _ = tiles.shape
    return pl.pallas_call(
        place_kernel,
        grid_spec=pltpu.PrefetchScalarGridSpec(
            num_scalar_prefetch=1,
            grid=(count,),
            in_specs=[pl.BlockSpec((1, size, size), lambda b, source: (source[b], 0, 0))],
            out_specs=pl.BlockSpec((size, size), lambda b, source: (0, b)),
        ),
        out_shape=jax.ShapeDtypeStruct((size, count * size), jnp.float32),
        name="place",
    )(inverse, tiles)


def finish_kernel(flags, part_ref, root_ref, panel_ref, own_ref, out_ref, turned_ref):
    width, columns = out_ref.shape
    size = panel_ref.shape[1]
    turned_ref[...] = panel_ref[...].T
    change = product(own_ref[...], turned_ref[...])
    mine = turned_ref[pl.ds(pl.multiple_of(flags[2] * width, width), width), :]
    first = flags[0] * size - pl.program_id(0) * columns
    lanes = lax.broadcasted_iota(jnp.int32, (width, columns), 1)
    dead = (lanes >= first) & (lanes < first + size)
    part = jnp.where(dead, 0.0, part_ref[...] + root_ref[...] - change)
    out_ref[...] = jnp.where(flags[0] == flags[1], mine, part)


def finish(part, root_rows, panel, flags):
    width, rows = part.shape
    size = panel.shape[1]
    chunk = 4 * size
    across = pl.BlockSpec((width, chunk), lambda b, flags: (0, b))
    return pl.pallas_call(
        finish_kernel,
        grid_spec=pltpu.PrefetchScalarGridSpec(
            num_scalar_prefetch=1,
            grid=(rows // chunk,),
            in_specs=[
                across,
                across,
                pl.BlockSpec((chunk, size), lambda b, flags: (b, 0)),
                pl.BlockSpec((width, size), lambda b, flags: (flags[3], 0)),
            ],
            out_specs=across,
            scratch_shapes=[pltpu.VMEM((size, chunk), jnp.float32)],
        ),
        out_shape=jax.ShapeDtypeStruct((width, rows), jnp.float32),
        name="finish",
    )(flags, part, root_rows, panel, panel)


def block_row(tiles, pivot_block):
    return lax.dynamic_index_in_dim(tiles, pivot_block, 0, keepdims=False)


def shards(leaf_fronts, root_front, leaf_order, leaf_map, root_order):
    order_rows, block_size = leaf_fronts.shape
    block_count = order_rows // block_size
    my_block = lax.axis_index("front").astype(jnp.int32)
    leaf_index = lax.axis_index("leaf").astype(jnp.int32)
    slice_width = root_front.shape[2]
    block_ids = jnp.arange(block_count, dtype=jnp.int32)

    tiles = leaf_fronts.reshape(block_count, block_size, block_size)
    first, second = leaf_order[0, 0], leaf_order[0, 1]
    inverse = invert(leaf_map[0])
    pivot = root_order[0]
    source = inverse[pivot]
    row_first = block_row(tiles, first).T
    row_second = block_row(tiles, second).T
    row_source = block_row(tiles, source).T
    raw_first = lax.all_gather(row_first, "front", axis=0, tiled=True)
    raw_first, row_second = lax.optimization_barrier((raw_first, row_second))
    raw_second = lax.all_gather(row_second, "front", axis=0, tiled=True)
    everything = jnp.ones((block_count,), dtype=jnp.bool_)
    panel_first = make_panel(raw_first, first, everything)
    root_rows = root_front[:, 0, :].T
    raw_second, root_rows, row_source, panel_first = lax.optimization_barrier(
        (raw_second, root_rows, row_source, panel_first)
    )
    raw_source = lax.all_gather(row_source, "front", axis=0, tiled=True)
    panel_second = make_panel(raw_second, second, block_ids != first, panel_first)

    flags = jnp.stack([first, second, my_block])
    leaf_out, outgoing = update(leaf_fronts, panel_first, panel_second, flags, leaf_map[0])
    raw_source, outgoing = lax.optimization_barrier((raw_source, outgoing))

    into = inverse[my_block]
    rows_of = lambda panel, block: lax.dynamic_slice_in_dim(
        panel, block * block_size, block_size, 0
    )
    share = rows_of(raw_source, into)
    for panel in (panel_first, panel_second):
        share = share - jnp.dot(rows_of(panel, into), rows_of(panel, source).T, precision=HIGH)
    live = (into != first) & (into != second) & (source != first) & (source != second)
    share = jnp.where(live, share, 0.0)
    root_share = lax.dynamic_slice_in_dim(root_rows, pivot * block_size, block_size, 1)
    here = leaf_index * slice_width
    widened = jnp.zeros_like(share)
    widened = lax.dynamic_update_slice_in_dim(widened, root_share, here, 0)
    shares = lax.all_gather(share + widened, "leaf", axis=0)
    shares, outgoing = lax.optimization_barrier((shares, outgoing))
    raw_root = jnp.sum(shares, axis=0)
    raw_root = lax.all_gather(raw_root, "front", axis=0, tiled=True)
    incoming = lax.all_to_all(outgoing, "front", split_axis=0, concat_axis=0, tiled=True)
    gathered = place_tiles(incoming, inverse)
    gathered, raw_root = lax.optimization_barrier((gathered, raw_root))
    part = lax.psum_scatter(gathered, "leaf", scatter_dimension=0, tiled=True)

    panel = make_panel(raw_root, pivot, everything)
    own_rows = my_block * (block_size // slice_width) + leaf_index
    ends = jnp.stack([pivot, my_block, leaf_index, own_rows])
    root_out = finish(part, root_rows, panel, ends).T
    return (leaf_out, root_out[:, None, :])


def solution(mesh):
    return jax.shard_map(
        shards,
        mesh=mesh,
        in_specs=(
            P("leaf", "front"),
            P(None, "front", "leaf"),
            P("leaf", None),
            P("leaf", None),
            P(),
        ),
        out_specs=(P("leaf", "front"), P(None, "front", "leaf")),
        check_vma=False,
    )
```
